512 devices in a mesh: team: 32 (over x, y, core), rep: 16 (over z).
Axes of the slice: x: 4, y: 4, z: 16, core: 2. Of those that a mesh axis runs over, the one named last changes fastest.
Arguments:
- features: bfloat16 [16384, 1024], P(('team', 'rep')), may hold values from -6 to 6
- degree: int32 [16384], P(('team', 'rep')), may hold values from 4 to 16
- blocks: bfloat16 [128, 16, 8, 128, 128], P('team', 'rep'), may hold values from -3 to 3
- block_cols: int32 [128, 16, 8], P('team', 'rep'), may hold values from 0 to 7, each once within a row
- block_count: int32 [128, 16], P('team', 'rep'), may hold values from 1 to 8, as said below
Outputs:
- hop1: bfloat16 [16384, 1024], P(('team', 'rep'))
- hop2: bfloat16 [16384, 1024], P(('team', 'rep'))
- hop3: bfloat16 [16384, 1024], P(('team', 'rep'))
The draws below stay inside these ranges and needn't reach their ends.
Inputs may be any that keep to these rules, and one draw needn't show every extreme that they name: Each of the 8 entries of a row of block_cols names a different column block; only the first block_count entries are used. `block_count`: some block row of some replica uses all 8 of its blocks.
All inputs are finite; a program needn't handle non-finite values.
Results may differ from the reference program's by a relative error of at most 0.04.
Values may be sent and summed in bfloat16 or wider, within the bound.
No kernel may reach another device: no remote copies, remote signals or barrier semaphores. Data moves between devices by JAX's collectives and lax.ppermute only.
A program may use at most 64 MiB of HBM per device.

```python
import jax
import jax.numpy as jnp
from jax import lax

F = 1024
BLK = 128
HOPS = 3
ROWS = 32
NODES = 16384
NBR = 128
CBLK = 8
N_TEAM = 32
N_REP = 16


def draw_block_count(key, part):
    first, second, third = jax.random.split(key, 3)
    left = jax.random.randint(first, (NBR, N_REP), 1, CBLK + 1)
    right = jax.random.randint(second, (NBR, N_REP), 1, CBLK + 1)
    counts = jnp.minimum(left, right).reshape(-1)
    chosen = jax.random.randint(third, (), 0, NBR * N_REP)
    counts = counts.at[chosen].set(CBLK)
    return counts.reshape(NBR, N_REP).astype(jnp.int32)


def place_ends(entries, stream_key, least, top_value):
    index_at = [jax.random.randint(jax.random.fold_in(stream_key, axis), (), 0, length) for axis, length in enumerate(entries.shape)]
    main_axis = entries.shape.index(max(entries.shape))
    beside = index_at[:main_axis] + [(index_at[main_axis] + 1) % entries.shape[main_axis]] + index_at[main_axis + 1:]
    return entries.at[tuple(index_at)].set(least).at[tuple(beside)].set(top_value)


def steps_of(own_key, dims, cuts, smallest, top_value):
    def one(dim, shards_of):
        draws = jax.random.uniform(jax.random.fold_in(jax.random.fold_in(own_key, 6), dim), (shards_of,), jnp.float32, smallest / len(cuts), top_value / len(cuts))
        return jnp.repeat(jnp.exp(draws), dims[dim] // shards_of).reshape((-1,) + (1,) * (len(dims) - dim - 1))

    factor_of = one(*cuts[0])
    for cut in cuts[1:]:
        factor_of = factor_of * one(*cut)
    return factor_of


def noise(rng, extent, width, limit, pieces=(), kind=jnp.bfloat16):
    values = jax.random.normal(rng, extent, jnp.float32) * width
    if len(pieces) > 0:
        values = steps_of(rng, extent, pieces, -0.22, 0.18) * values
    return jnp.clip(values, min=-limit, max=limit).astype(kind)


def setup_inputs(seed: int = 0) -> dict:
    seeds = jax.random.split(jax.random.key(seed), 6)
    features = noise(seeds[0], (NODES, F), 1.0, 6.0, ((0, 512),))
    degree = place_ends(jax.random.randint(seeds[1], (NODES,), 4, 17), jax.random.fold_in(seeds[1], 1), 4, 16).astype(jnp.int32)
    blocks = noise(seeds[2], (NBR, N_REP, CBLK, BLK, BLK), 0.5, 3.0, ((0, 32), (1, 16)))
    block_cols = jax.vmap(lambda own: jax.random.permutation(own, CBLK))(jax.random.split(seeds[3], NBR * N_REP)).reshape((NBR, N_REP, CBLK)).astype(jnp.int32)
    block_count = draw_block_count(jax.random.fold_in(seeds[5], 71), 0)
    return {"features": features, "degree": degree, "blocks": blocks, "block_cols": block_cols, "block_count": block_count}


def reference(features, degree, blocks, block_cols, block_count):
    scale = lax.rsqrt(degree.astype(jnp.float32))[:, None]
    slots = jnp.arange(CBLK)
    picks = (block_cols[..., None] == slots[None, None, None, :]) & (slots[None, None, :, None] < block_count[:, :, None, None])
    picks = picks.astype(jnp.float32)
    current = features
    results = []
    for hop in range(HOPS):
        sent = (scale * current.astype(jnp.float32)).astype(jnp.bfloat16)
        sent = lax.optimization_barrier(sent)
        sent_wide = sent.astype(jnp.float32)
        grouped = sent_wide.reshape(N_TEAM, N_REP, ROWS, F)

        def add_replica(replica, total):
            columns = lax.dynamic_index_in_dim(grouped, replica, 1, keepdims=False).reshape(N_TEAM * ROWS, F)
            tiles = lax.dynamic_index_in_dim(blocks, replica, 1, keepdims=False).astype(jnp.float32)
            chosen = lax.dynamic_index_in_dim(picks, replica, 1, keepdims=False)
            dense = jnp.einsum('gtuv,gtb->gubv', tiles, chosen, precision=lax.Precision.HIGHEST)
            dense = dense.reshape(NODES, CBLK * BLK)
            partial_value = jnp.dot(dense, columns, precision=lax.Precision.HIGHEST, preferred_element_type=jnp.float32)
            partial_value = lax.optimization_barrier(partial_value.astype(jnp.bfloat16)).astype(jnp.float32)
            return total + partial_value
        total = lax.fori_loop(0, N_REP, add_replica, jnp.zeros((NODES, F), jnp.float32))
        current = (scale * (total + sent_wide)).astype(jnp.bfloat16)
        results.append(current)
    return (results[0], results[1], results[2])
```

```python
import jax
import jax.numpy as jnp
from jax import lax
from jax.experimental import pallas as pl
from jax.experimental.pallas import tpu as pltpu
from jax.sharding import Mesh, PartitionSpec as P

HOPS = 3
PLANE = ("x", "y")
FAR = ("zh", "zm")
POOL = ("c", "z0")
SIZES = {"x": 4, "y": 4, "c": 2, "zh": 4, "zm": 2, "z0": 2}
VMEM = pl.BlockSpec(memory_space=pltpu.VMEM)
SMEM = pl.BlockSpec(memory_space=pltpu.SMEM)


def exchange(x, axes):
    return lax.all_to_all(x, axes, 0, 0, tiled=True)


def swap(x, axis):
    return lax.ppermute(x, axis, [(0, 1), (1, 0)])


def dense_kernel(cols, counts, blocks, out):
    out[...] = jnp.zeros_like(out)
    row_blocks, slots, size, _ = blocks.shape
    for g in range(row_blocks):
        for t in range(slots):

            @pl.when(t < counts[g])
            def _():
                at = pl.multiple_of(cols[g, t] * size, size)
                out[g * size : (g + 1) * size, pl.ds(at, size)] = blocks[g, t]


def build_dense(blocks, cols, counts):
    g, t, size, _ = blocks.shape
    return pl.pallas_call(
        dense_kernel,
        out_shape=jax.ShapeDtypeStruct((g * size, t * size), blocks.dtype),
        in_specs=[SMEM, SMEM, VMEM],
        out_specs=VMEM,
        name="dense_panel",
    )(cols, counts, blocks)


def first_kernel(got, sent, copies, scale):
    pool, rows, width = got.shape
    wide = width - 128
    for q in range(pool):
        s = lax.rsqrt(got[q, :, wide:].astype(jnp.float32))
        s = jnp.concatenate([s] * (wide // 128), axis=1)
        scale[q * rows : (q + 1) * rows, :] = s
        value = (s * got[q, :, :wide].astype(jnp.float32)).astype(jnp.bfloat16)
        sent[q * rows : (q + 1) * rows, :] = value
        for k in range(copies.shape[0]):
            copies[k, q * rows : (q + 1) * rows, :] = value


def first(got, n_copies):
    pool, rows, width = got.shape
    wide = width - 128
    shape = (pool * rows, wide)
    return pl.pallas_call(
        first_kernel,
        out_shape=(
            jax.ShapeDtypeStruct(shape, jnp.bfloat16),
            jax.ShapeDtypeStruct((n_copies,) + shape, jnp.bfloat16),
            jax.ShapeDtypeStruct(shape, jnp.float32),
        ),
        in_specs=[VMEM],
        out_specs=(VMEM, VMEM, VMEM),
        name="first_scale",
    )(got)


def product_kernel(place, whole, a00, a01, a10, a11, out, columns):
    plane, pair, rows, _ = whole.shape
    far = out.shape[0]
    for j in range(plane):
        for z in range(pair):
            columns[z, j * rows : (j + 1) * rows, :] = whole[j, z]
    core, level = place[0], place[1]
    mine = columns[level]
    other = columns[1 - level]
    for near, (ours, theirs) in enumerate(((a00, a01), (a10, a11))):
        value = jnp.dot(ours[...], mine, preferred_element_type=jnp.float32)
        value += jnp.dot(theirs[...], other, preferred_element_type=jnp.float32)
        value = value.astype(jnp.bfloat16).reshape(far, pair, rows // 2, -1)
        target = core if near == 0 else 1 - core
        for z in range(pair):
            out[:, z, target] = value[:, z]


def product(place, whole, panels, far):
    plane, pair, rows, width = whole.shape
    return pl.pallas_call(
        product_kernel,
        out_shape=jax.ShapeDtypeStruct((far, pair, 2, rows // 2, width), jnp.bfloat16),
        in_specs=[SMEM] + [VMEM] * 5,
        out_specs=VMEM,
        scratch_shapes=[pltpu.VMEM((pair, plane * rows, width), jnp.bfloat16)],
        compiler_params=pltpu.CompilerParams(vmem_limit_bytes=40 << 20),
        name="panel_product",
    )(place, whole, *panels)


def update_kernel(parts, sent, scale, hop, new_sent, copies):
    total = parts[0].astype(jnp.float32)
    for k in range(1, parts.shape[0]):
        total += parts[k].astype(jnp.float32)
    s = scale[...]
    value = (s * (total + sent[...].astype(jnp.float32))).astype(jnp.bfloat16)
    hop[...] = value
    value = (s * value.astype(jnp.float32)).astype(jnp.bfloat16)
    new_sent[...] = value
    for k in range(copies.shape[0]):
        copies[k] = value


def update(parts, sent, scale, n_copies):
    shape = sent.shape
    return pl.pallas_call(
        update_kernel,
        out_shape=(
            jax.ShapeDtypeStruct(shape, jnp.bfloat16),
            jax.ShapeDtypeStruct(shape, jnp.bfloat16),
            jax.ShapeDtypeStruct((n_copies,) + shape, jnp.bfloat16),
        ),
        in_specs=[VMEM] * 3,
        out_specs=(VMEM,) * 3,
        name="update",
    )(parts, sent, scale)


def last_kernel(parts, sent, scale, hop):
    total = parts[0].astype(jnp.float32)
    for k in range(1, parts.shape[0]):
        total += parts[k].astype(jnp.float32)
    value = scale[...] * (total + sent[...].astype(jnp.float32))
    hop[...] = value.astype(jnp.bfloat16)


def last(parts, sent, scale):
    return pl.pallas_call(
        last_kernel,
        out_shape=jax.ShapeDtypeStruct(sent.shape, jnp.bfloat16),
        in_specs=[VMEM] * 3,
        out_specs=VMEM,
        name="last_update",
    )(parts, sent, scale)


def on_device(features, degree, blocks, block_cols, block_count):
    rows, full = features.shape
    pool = SIZES["c"] * SIZES["z0"]
    far = SIZES["zh"] * SIZES["zm"]
    plane = SIZES["x"] * SIZES["y"]
    width = full // pool
    place = jnp.stack([lax.axis_index("c"), lax.axis_index("z0")]).astype(jnp.int32)

    slices = features.reshape(rows, pool, width).transpose(1, 0, 2)
    counts = jnp.broadcast_to(degree.astype(jnp.bfloat16)[None, :, None], (pool, rows, 128))
    got = exchange(jnp.concatenate([slices, counts], axis=2), ("z0", "c"))
    sent, copies, scale = first(got, plane)

    a00 = build_dense(blocks[:, 0], block_cols[:, 0], block_count[:, 0])
    a01 = swap(a00, "z0")
    a10 = swap(a00, "c")
    a11 = swap(a01, "c")
    panels = (a00, a01, a10, a11)

    hops = []
    for hop in range(HOPS):
        whole = exchange(copies, PLANE).reshape(plane, 2, 2 * rows, width)
        partial_value = product(place, whole, panels, far)
        parts = exchange(partial_value.reshape(far, pool * rows, width), FAR)
        if hop < HOPS - 1:
            value, sent, copies = update(parts, sent, scale, plane)
        else:
            value = last(parts, sent, scale)
        hops.append(value.reshape(pool, rows, width))
    back = exchange(jnp.stack(hops, axis=1), ("z0", "c"))
    return tuple(
        back[:, k].transpose(1, 0, 2).reshape(rows, full) for k in range(HOPS)
    )


def solution(mesh):
    axes = tuple(SIZES)
    fine = Mesh(mesh.devices.reshape(tuple(SIZES.values())), axes)
    in_specs = (
        P(axes, None),
        P(axes),
        P(axes[:3], axes[3:], None, None, None),
        P(axes[:3], axes[3:], None),
        P(axes[:3], axes[3:]),
    )
    out_specs = (P(axes, None),) * 3
    return jax.shard_map(
        on_device, mesh=fine, in_specs=in_specs, out_specs=out_specs, check_vma=False
    )
```

```python
import jax
import jax.numpy as jnp
from jax import lax
from jax.experimental import pallas as pl
from jax.experimental.pallas import tpu as pltpu
from jax.sharding import Mesh, PartitionSpec as P

HOPS = 3
SIZES = {"x": 4, "y": 4, "c": 2, "zh": 4, "zl": 4}
PLANE = ("x", "y")
LINE = ("zh", "zl")
LENGTH = 16
WINDOW = 4
LANES = 128
VMEM = pl.BlockSpec(memory_space=pltpu.VMEM)
SMEM = pl.BlockSpec(memory_space=pltpu.SMEM)


def exchange(x, axes):
    return lax.all_to_all(x, axes, 0, 0, tiled=True)


def send(x, step):
    return lax.ppermute(x, LINE, [(i, (i + step) % LENGTH) for i in range(LENGTH)])


def swap_cores(x):
    return lax.ppermute(x, "c", [(0, 1), (1, 0)])


def struct(shape, dtype=jnp.bfloat16):
    return jax.ShapeDtypeStruct(shape, dtype)


def dense_kernel(cols, counts, blocks, out):
    out[...] = jnp.zeros_like(out)
    row_blocks, slots, size, _ = blocks.shape
    for g in range(row_blocks):
        for t in range(slots):

            @pl.when(t < counts[g])
            def _():
                at = pl.multiple_of(cols[g, t] * size, size)
                out[g * size : (g + 1) * size, pl.ds(at, size)] = blocks[g, t]


def build_dense(blocks, cols, counts):
    g, t, size, _ = blocks.shape
    return pl.pallas_call(
        dense_kernel,
        out_shape=struct((g * size, t * size)),
        in_specs=[SMEM, SMEM, VMEM],
        out_specs=VMEM,
        name="dense_panel",
    )(cols, counts, blocks)


def spread_kernel(place, features, degree, own, ahead, back, back2):
    width = features.shape[1] // WINDOW
    for step, out in ((0, own), (1, ahead), (-1, back), (-2, back2)):
        piece = lax.rem(place[1] + step + WINDOW, WINDOW)
        at = pl.multiple_of(piece * width, width)
        out[:, :width] = features[:, pl.ds(at, width)]
        out[:, width:] = degree[...]


def spread(place, features, degree):
    rows, full = features.shape
    shape = struct((rows, full // WINDOW + LANES))
    return pl.pallas_call(
        spread_kernel,
        out_shape=(shape,) * 4,
        in_specs=[SMEM, VMEM, VMEM],
        out_specs=(VMEM,) * 4,
        name="spread_rows",
    )(place, features, degree)


def first_kernel(*refs):
    sent, copies, scale = refs[WINDOW:]
    rows, width = refs[0].shape
    width -= LANES
    for w, got in enumerate(refs[:WINDOW]):
        at = slice(w * rows, (w + 1) * rows)
        s = lax.rsqrt(got[:, width:].astype(jnp.float32))
        s = jnp.concatenate([s] * (width // LANES), axis=1)
        value = (s * got[:, :width].astype(jnp.float32)).astype(jnp.bfloat16)
        scale[at, :] = s
        sent[at, :] = value
        for k in range(copies.shape[0]):
            copies[k, at, :] = value


def first(pieces, n_copies):
    rows, width = pieces[0].shape
    shape = (WINDOW * rows, width - LANES)
    return pl.pallas_call(
        first_kernel,
        out_shape=(struct(shape), struct((n_copies,) + shape), struct(shape, jnp.float32)),
        in_specs=[VMEM] * WINDOW,
        out_specs=(VMEM,) * 3,
        name="first_scale",
    )(*pieces)


def product_kernel(place, ours, theirs, p0, p1, p2, p3, out, columns):
    core, level = place[0], place[1]
    plane, rows, width = ours.shape
    rows //= WINDOW
    for j in range(plane):
        for w in range(WINDOW):
            columns[w, j, core] = ours[j, w * rows : (w + 1) * rows]
            columns[w, j, 1 - core] = theirs[j, w * rows : (w + 1) * rows]
    total = None
    for w, panel in enumerate((p0, p1, p2, p3)):
        value = jnp.dot(
            panel[...], columns[w].reshape(-1, width), preferred_element_type=jnp.float32
        )
        total = value if total is None else total + value
    total = total.astype(jnp.bfloat16).reshape(LENGTH, rows, width)
    for r in range(LENGTH):
        out[lax.rem(r + 1 + LENGTH - level, LENGTH)] = total[r]


def product(place, ours, theirs, panels):
    plane, rows, width = ours.shape
    rows //= WINDOW
    return pl.pallas_call(
        product_kernel,
        out_shape=struct((LENGTH, rows, width)),
        in_specs=[SMEM] + [VMEM] * 6,
        out_specs=VMEM,
        scratch_shapes=[pltpu.VMEM((WINDOW, plane, 2, rows, width), jnp.bfloat16)],
        compiler_params=pltpu.CompilerParams(vmem_limit_bytes=40 << 20),
        name="panel_product",
    )(place, ours, theirs, *panels)


def update_kernel(parts, sent, scale, hop, *more):
    total = parts[0].astype(jnp.float32)
    for k in range(1, parts.shape[0]):
        total += parts[k].astype(jnp.float32)
    s = scale[...]
    value = (s * (total + sent[...].astype(jnp.float32))).astype(jnp.bfloat16)
    hop[...] = value
    if more:
        new_sent, copies = more
        value = (s * value.astype(jnp.float32)).astype(jnp.bfloat16)
        new_sent[...] = value
        for k in range(copies.shape[0]):
            copies[k] = value


def update(parts, sent, scale, n_copies):
    shape = struct(sent.shape)
    out = (shape, shape, struct((n_copies,) + sent.shape)) if n_copies else (shape,)
    return pl.pallas_call(
        update_kernel,
        out_shape=out,
        in_specs=[VMEM] * 3,
        out_specs=(VMEM,) * len(out),
        name="update",
    )(parts, sent, scale)


def collect_kernel(place, own, ahead, back, back2, *outs):
    width = own.shape[2]
    for step, got in ((0, own), (1, ahead), (-1, back), (-2, back2)):
        piece = lax.rem(place[1] + step + WINDOW, WINDOW)
        at = pl.multiple_of(piece * width, width)
        for k, out in enumerate(outs):
            out[:, pl.ds(at, width)] = got[k]


def collect(place, pieces):
    hops, rows, width = pieces[0].shape
    return pl.pallas_call(
        collect_kernel,
        out_shape=(struct((rows, WINDOW * width)),) * hops,
        in_specs=[SMEM] + [VMEM] * 4,
        out_specs=(VMEM,) * hops,
        name="collect_rows",
    )(place, *pieces)


def on_device(features, degree, blocks, block_cols, block_count):
    rows = features.shape[0]
    plane = SIZES["x"] * SIZES["y"]
    place = jnp.stack([lax.axis_index("c"), lax.axis_index("zl")]).astype(jnp.int32)

    wide = jnp.broadcast_to(degree.astype(jnp.bfloat16)[:, None], (rows, LANES))
    own, ahead, back, back2 = spread(place, features, wide)
    pieces = (send(ahead, 1), own, send(back, -1), send(back2, -2))
    sent, copies, scale = first(pieces, plane)

    panel = build_dense(blocks[:, 0], block_cols[:, 0], block_count[:, 0])
    above = send(panel, -1)
    below = send(panel, 1)
    gate, _ = lax.optimization_barrier((above, copies))
    panels = (below, panel, above, send(gate, -1))

    hops = []
    for hop in range(HOPS):
        ours = exchange(copies, PLANE)
        theirs = swap_cores(ours)
        partial_value = product(place, ours, theirs, panels)
        parts = exchange(partial_value.reshape(SIZES["zh"], WINDOW * rows, -1), "zh")
        value, *more = update(parts, sent, scale, plane if hop < HOPS - 1 else 0)
        if more:
            sent, copies = more
        hops.append(value.reshape(WINDOW, rows, -1))
    hops = jnp.stack(hops, axis=1)
    return collect(place, (hops[1], send(hops[0], -1), send(hops[2], 1), send(hops[3], 2)))


def solution(mesh):
    axes = tuple(SIZES)
    fine = Mesh(mesh.devices.reshape(tuple(SIZES.values())), axes)
    in_specs = (
        P(axes, None),
        P(axes),
        P(axes[:3], axes[3:], None, None, None),
        P(axes[:3], axes[3:], None),
        P(axes[:3], axes[3:]),
    )
    out_specs = (P(axes, None),) * 3
    return jax.shard_map(
        on_device, mesh=fine, in_specs=in_specs, out_specs=out_specs, check_vma=False
    )
```

```python
import jax
import jax.numpy as jnp
from jax import lax
from jax.experimental import pallas as pl
from jax.experimental.pallas import tpu as pltpu
from jax.sharding import Mesh, PartitionSpec as P

HOPS = 3
SIZES = {"x": 4, "y": 4, "c": 2, "zh": 4, "zl": 4}
PLANE = ("x", "y")
LINE = ("zh", "zl")
LENGTH = 16
WINDOW = 4
CORES = 2
LANES = 128
VMEM = pl.BlockSpec(memory_space=pltpu.VMEM)
SMEM = pl.BlockSpec(memory_space=pltpu.SMEM)


def exchange(x, axes):
    return lax.all_to_all(x, axes, 0, 0, tiled=True)


def send(x, step):
    return lax.ppermute(x, LINE, [(i, (i + step) % LENGTH) for i in range(LENGTH)])


def swap_cores(x):
    return lax.ppermute(x, "c", [(0, 1), (1, 0)])


def after(x, *others):
    return lax.optimization_barrier((x,) + others)[0]


def dense_kernel(cols, counts, blocks, out):
    out[...] = jnp.zeros_like(out)
    row_blocks, slots, size, _ = blocks.shape
    for g in range(row_blocks):
        for t in range(slots):

            @pl.when(t < counts[g])
            def _():
                at = pl.multiple_of(cols[g, t] * size, size)
                out[g * size : (g + 1) * size, pl.ds(at, size)] = blocks[g, t]


def build_dense(blocks, cols, counts):
    g, t, size, _ = blocks.shape
    return pl.pallas_call(
        dense_kernel,
        out_shape=jax.ShapeDtypeStruct((g * size, t * size), blocks.dtype),
        in_specs=[SMEM, SMEM, VMEM],
        out_specs=VMEM,
        name="dense_panel",
    )(cols, counts, blocks)


def product_kernel(place, whole, *refs):
    panels, (out, columns) = refs[: 2 * WINDOW], refs[2 * WINDOW :]
    core, level = place[0], place[1]
    plane, window, rows, width = whole.shape
    for j in range(plane):
        for w in range(window):
            columns[w, j] = whole[j, w]
    for near in range(CORES):
        total = None
        for w in range(window):
            value = jnp.dot(
                panels[near * window + w][...],
                columns[w].reshape(-1, width),
                preferred_element_type=jnp.float32,
            )
            total = value if total is None else total + value
        total = total.astype(jnp.bfloat16).reshape(LENGTH, rows // CORES, width)
        target = core if near == 0 else 1 - core
        for r in range(LENGTH):
            out[lax.rem(r + 1 + LENGTH - level, LENGTH), target] = total[r]


def product(place, whole, panels):
    plane, window, rows, width = whole.shape
    return pl.pallas_call(
        product_kernel,
        out_shape=jax.ShapeDtypeStruct((LENGTH, CORES, rows // CORES, width), jnp.bfloat16),
        in_specs=[SMEM] + [VMEM] * (1 + len(panels)),
        out_specs=VMEM,
        scratch_shapes=[pltpu.VMEM((window, plane, rows, width), jnp.bfloat16)],
        compiler_params=pltpu.CompilerParams(vmem_limit_bytes=40 << 20),
        name="panel_product",
    )(place, whole, *panels)


def on_device(features, degree, blocks, block_cols, block_count):
    f32, bf16 = jnp.float32, jnp.bfloat16
    rows, full = features.shape
    width = full // (CORES * WINDOW)
    plane = SIZES["x"] * SIZES["y"]
    pooled = WINDOW * CORES * rows
    level = lax.axis_index("zl")
    place = jnp.stack([lax.axis_index("c"), level]).astype(jnp.int32)

    panel = build_dense(blocks[:, 0], block_cols[:, 0], block_count[:, 0])
    above = send(panel, -1)
    below = send(panel, 1)

    half = full // CORES
    counts = jnp.broadcast_to(degree.astype(bf16)[:, None], (rows, LANES))
    halves = [jnp.concatenate([features[:, :half], counts], axis=1)]
    halves += [jnp.concatenate([features[:, half:], counts], axis=1)]
    got = exchange(jnp.stack(halves), "c")

    def piece(step):
        at = ((level + step) & (WINDOW - 1)) * width
        part = lax.dynamic_slice_in_dim(got, at, width, axis=2)
        return jnp.concatenate([part, got[:, :, half:]], axis=2)

    window = jnp.stack([send(piece(1), 1), piece(0), send(piece(-1), -1), send(piece(-2), -2)])
    window = window.reshape(pooled, width + LANES)
    scale = lax.rsqrt(window[:, width : width + 1].astype(f32))
    sent = (scale * window[:, :width].astype(f32)).astype(bf16)

    copies = jnp.broadcast_to(sent[None], (plane,) + sent.shape)
    two_above = send(after(above, below, copies), -1)
    whole = exchange(copies, PLANE)
    mine = (below, panel, above, two_above)
    early = tuple(swap_cores(p) for p in (after(below, copies), panel, after(above, copies)))
    panels = mine + early + (swap_cores(after(two_above, whole)),)

    hops = []
    for hop in range(HOPS):
        if hop:
            copies = jnp.broadcast_to(sent[None], (plane,) + sent.shape)
            whole = exchange(copies, PLANE)
        partial_value = product(
            place, whole.reshape(plane, WINDOW, CORES * rows, width), panels
        )
        parts = exchange(partial_value.reshape(SIZES["zh"], pooled, width), "zh")
        total = jnp.sum(parts.astype(f32), axis=0)
        value = (scale * (total + sent.astype(f32))).astype(bf16)
        sent = (scale * value.astype(f32)).astype(bf16)
        hops.append(value.reshape(WINDOW, CORES, rows, width))

    both = jnp.stack(hops, axis=2)
    arrived = (both[1], send(both[0], -1), send(both[3], 2), send(both[2], 1))
    turned = jnp.zeros((WINDOW,) + both.shape[1:], bf16)
    for step, part in enumerate(arrived):
        turned = lax.dynamic_update_index_in_dim(turned, part, (level + step) & (WINDOW - 1), 0)
    back = exchange(turned.transpose(1, 0, 2, 3, 4), "c")
    return tuple(
        jnp.concatenate([back[c, q, k] for c in range(CORES) for q in range(WINDOW)], axis=1)
        for k in range(HOPS)
    )


def solution(mesh):
    axes = tuple(SIZES)
    fine = Mesh(mesh.devices.reshape(tuple(SIZES.values())), axes)
    in_specs = (
        P(axes, None),
        P(axes),
        P(axes[:3], axes[3:], None, None, None),
        P(axes[:3], axes[3:], None),
        P(axes[:3], axes[3:]),
    )
    out_specs = (P(axes, None),) * 3
    return jax.shard_map(
        on_device, mesh=fine, in_specs=in_specs, out_specs=out_specs, check_vma=False
    )
```

```python
import jax
import jax.numpy as jnp
from jax import lax
from jax.experimental import pallas as pl
from jax.experimental.pallas import tpu as pltpu
from jax.sharding import Mesh, PartitionSpec as P

HOPS = 3
SIZES = {"x": 4, "y": 4, "c": 2, "zhalf": 2, "zquad": 4, "zodd": 2}
PLANE = ("x", "y")
LINE = ("zhalf", "zquad", "zodd")
POOL = ("zodd", "c")
PAIRS = 8
GROUPS = [
    [2 * k + (s if k < PAIRS // 2 else 1 - s) for k in range(PAIRS)] for s in range(2)
]
LANES = 128
VMEM = pl.BlockSpec(memory_space=pltpu.VMEM)
SMEM = pl.BlockSpec(memory_space=pltpu.SMEM)


def exchange(x, axes, groups=None):
    return lax.all_to_all(x, axes, 0, 0, tiled=True, axis_index_groups=groups)


def swap(x, axis):
    return lax.ppermute(x, axis, [(0, 1), (1, 0)])


def after(x, *others):
    return lax.optimization_barrier((x,) + others)[0]


def dense_kernel(cols, counts, blocks, out):
    out[...] = jnp.zeros_like(out)
    row_blocks, slots, size, _ = blocks.shape
    for g in range(row_blocks):
        for t in range(slots):

            @pl.when(t < counts[g])
            def _():
                at = pl.multiple_of(cols[g, t] * size, size)
                out[g * size : (g + 1) * size, pl.ds(at, size)] = blocks[g, t]


def build_dense(blocks, cols, counts):
    g, t, size, _ = blocks.shape
    return pl.pallas_call(
        dense_kernel,
        out_shape=jax.ShapeDtypeStruct((g * size, t * size), blocks.dtype),
        in_specs=[SMEM, SMEM, VMEM],
        out_specs=VMEM,
        compiler_params=pltpu.CompilerParams(vmem_limit_bytes=8 << 20),
        name="dense_panel",
    )(cols, counts, blocks)


def product_kernel(place, whole, a00, a01, a10, a11, out, columns):
    core, level = place[0], place[1]
    plane, pair, rows, width = whole.shape
    for j in range(plane):
        for z in range(pair):
            columns[z, j] = whole[j, z]
    for near, (ours, theirs) in enumerate(((a00, a01), (a10, a11))):
        value = jnp.dot(
            ours[...], columns[level].reshape(-1, width), preferred_element_type=jnp.float32
        )
        value += jnp.dot(
            theirs[...], columns[1 - level].reshape(-1, width), preferred_element_type=jnp.float32
        )
        value = value.astype(jnp.bfloat16).reshape(PAIRS, pair, rows // 2, width)
        target = core if near == 0 else 1 - core
        for z in range(pair):
            out[:, z, target] = value[:, z]


def product(place, whole, panels):
    plane, pair, rows, width = whole.shape
    return pl.pallas_call(
        product_kernel,
        out_shape=jax.ShapeDtypeStruct((PAIRS, pair, 2, rows // 2, width), jnp.bfloat16),
        in_specs=[SMEM] + [VMEM] * 5,
        out_specs=VMEM,
        scratch_shapes=[pltpu.VMEM((pair, plane, rows, width), jnp.bfloat16)],
        compiler_params=pltpu.CompilerParams(vmem_limit_bytes=14 << 20),
        name="panel_product",
    )(place, whole, *panels)


def on_device(features, degree, blocks, block_cols, block_count):
    f32, bf16 = jnp.float32, jnp.bfloat16
    rows, full = features.shape
    width = full // 4
    pooled = 4 * rows
    plane = SIZES["x"] * SIZES["y"]
    place = jnp.stack([lax.axis_index("c"), lax.axis_index("zodd")]).astype(jnp.int32)
    crossed = lax.axis_index("zhalf") == 1

    counts = jnp.broadcast_to(degree.astype(bf16)[:, None], (rows, LANES))
    slices = jnp.stack(
        [
            jnp.concatenate([features[:, q * width : (q + 1) * width], counts], axis=1)
            for q in range(4)
        ]
    )
    slices = jnp.where(crossed, jnp.roll(slices, 2, axis=0), slices)
    got = exchange(slices, POOL).reshape(pooled, width + LANES)
    scale = lax.rsqrt(got[:, width : width + 1].astype(f32))
    sent = (scale * got[:, :width].astype(f32)).astype(bf16)
    copies = jnp.broadcast_to(sent[None], (plane,) + sent.shape)
    whole = exchange(copies, PLANE)

    blocks, block_cols = lax.optimization_barrier((blocks, block_cols, slices))[:2]
    a00 = build_dense(blocks[:, 0], block_cols[:, 0], block_count[:, 0])
    a01 = swap(a00, "zodd")
    a10 = swap(a00, "c")
    a11 = swap(after(a01, whole), "c")
    panels = (a00, a01, a10, a11)

    hops = []
    for hop in range(HOPS):
        if hop:
            copies = jnp.broadcast_to(sent[None], (plane,) + sent.shape)
            whole = exchange(copies, PLANE)
        partial_value = product(place, whole.reshape(plane, 2, 2 * rows, width), panels)
        parts = exchange(partial_value.reshape(PAIRS, pooled, width), LINE, GROUPS)
        total = jnp.sum(parts.astype(f32), axis=0)
        value = (scale * (total + sent.astype(f32))).astype(bf16)
        sent = (scale * value.astype(f32)).astype(bf16)
        hops.append(value.reshape(4, rows, width))
    back = exchange(jnp.stack(hops, axis=1), POOL)
    back = jnp.where(crossed, jnp.roll(back, 2, axis=0), back)
    return tuple(
        back[:, k].transpose(1, 0, 2).reshape(rows, full) for k in range(HOPS)
    )


def solution(mesh):
    axes = tuple(SIZES)
    fine = Mesh(mesh.devices.reshape(tuple(SIZES.values())), axes)
    in_specs = (
        P(axes, None),
        P(axes),
        P(axes[:3], axes[3:], None, None, None),
        P(axes[:3], axes[3:], None),
        P(axes[:3], axes[3:]),
    )
    out_specs = (P(axes, None),) * 3
    return jax.shard_map(
        on_device, mesh=fine, in_specs=in_specs, out_specs=out_specs, check_vma=False
    )
```

```python
import jax
import jax.numpy as jnp
from jax import lax
from jax.experimental import pallas as pl
from jax.experimental.pallas import tpu as pltpu
from jax.sharding import Mesh, PartitionSpec as P

HOPS = 3
SIZES = {"x": 4, "y": 4, "c": 2, "z": 16}
PLANE = ("x", "y")
LENGTH = 16
TILES = LENGTH // 2
STEP = 4
TILE_GROUPS = [
    [core * LENGTH + 2 * k + level for level in range(2) for core in range(2)] for k in range(TILES)
]
NEIGHBOURS = [(z, (z + 1 if z % 2 else z - 1) % LENGTH) for z in range(LENGTH)]
SUM_GROUPS = [
    [(STEP * k + first + (side if k < STEP // 2 else 1 - side)) % LENGTH for k in range(STEP)]
    for first in (1, 3)
    for side in range(2)
]


def tile_places():
    group_of = {z: group for group in SUM_GROUPS for z in group}
    return [
        [[z // 2 for z in group_of[me] + group_of[other]].index(k) for k in range(TILES)]
        for me, other in NEIGHBOURS
    ]


LANES = 128
CORES = [(0, 1), (1, 0)]
LEVELS = [(z, z ^ 1) for z in range(LENGTH)]
VMEM = pl.BlockSpec(memory_space=pltpu.VMEM)
SMEM = pl.BlockSpec(memory_space=pltpu.SMEM)


def exchange(x, axes, groups=None):
    return lax.all_to_all(x, axes, 0, 0, tiled=True, axis_index_groups=groups)


def swap(x, axis, pairs):
    return lax.ppermute(x, axis, pairs)


def after(x, *others):
    return lax.optimization_barrier((x,) + others)[0]


def dense_kernel(cols, counts, blocks, out):
    out[...] = jnp.zeros_like(out)
    row_blocks, slots, size, _ = blocks.shape
    for g in range(row_blocks):
        for t in range(slots):

            @pl.when(t < counts[g])
            def _():
                at = pl.multiple_of(cols[g, t] * size, size)
                out[g * size : (g + 1) * size, pl.ds(at, size)] = blocks[g, t]


def build_dense(blocks, cols, counts):
    g, t, size, _ = blocks.shape
    return pl.pallas_call(
        dense_kernel,
        out_shape=jax.ShapeDtypeStruct((g * size, t * size), blocks.dtype),
        in_specs=[SMEM, SMEM, VMEM],
        out_specs=VMEM,
        compiler_params=pltpu.CompilerParams(vmem_limit_bytes=8 << 20),
        name="dense_panel",
    )(cols, counts, blocks)


def product_kernel(place, whole, a00, a01, a10, a11, stay, go, columns, tiles):
    core, level = place[0], place[1]
    plane, pair, rows, width = whole.shape
    for j in range(plane):
        for z in range(pair):
            columns[z, j] = whole[j, z]
    for near, (ours, theirs) in enumerate(((a00, a01), (a10, a11))):
        value = jnp.dot(
            ours[...], columns[level].reshape(-1, width), preferred_element_type=jnp.float32
        )
        value += jnp.dot(
            theirs[...], columns[1 - level].reshape(-1, width), preferred_element_type=jnp.float32
        )
        value = value.astype(jnp.bfloat16).reshape(TILES, pair, rows // 2, width)
        target = core if near == 0 else 1 - core
        for k in range(TILES):
            for z in range(pair):
                tiles[place[2 + k], z, target] = value[k, z]
    stay[...] = tiles[:STEP]
    go[...] = tiles[STEP:]


def product(place, whole, panels):
    plane, pair, rows, width = whole.shape
    part = (pair, 2, rows // 2, width)
    half = jax.ShapeDtypeStruct((STEP,) + part, jnp.bfloat16)
    return pl.pallas_call(
        product_kernel,
        out_shape=(half, half),
        in_specs=[SMEM] + [VMEM] * 5,
        out_specs=(VMEM, VMEM),
        scratch_shapes=[
            pltpu.VMEM((pair, plane, rows, width), jnp.bfloat16),
            pltpu.VMEM((TILES,) + part, jnp.bfloat16),
        ],
        compiler_params=pltpu.CompilerParams(vmem_limit_bytes=14 << 20),
        name="panel_product",
    )(place, whole, *panels)


def on_device(features, degree, blocks, block_cols, block_count):
    f32, bf16 = jnp.float32, jnp.bfloat16
    rows, full = features.shape
    width = full // 4
    pooled = 4 * rows
    plane = SIZES["x"] * SIZES["y"]
    z = lax.axis_index("z")
    here = jnp.stack([lax.axis_index("c"), z & 1]).astype(jnp.int32)
    place = jnp.concatenate([here, jnp.asarray(tile_places(), jnp.int32)[z]])
    crossed = (z & 2) != 0

    counts = jnp.broadcast_to(degree.astype(bf16)[:, None], (rows, LANES))
    slices = jnp.stack(
        [
            jnp.concatenate([features[:, q * width : (q + 1) * width], counts], axis=1)
            for q in range(4)
        ]
    )
    slices = jnp.where(crossed, jnp.roll(slices, 2, axis=0), slices)
    got = exchange(slices, ("c", "z"), TILE_GROUPS).reshape(pooled, width + LANES)
    scale = lax.rsqrt(got[:, width : width + 1].astype(f32))
    sent = (scale * got[:, :width].astype(f32)).astype(bf16)
    copies = jnp.broadcast_to(sent[None], (plane,) + sent.shape)
    whole = exchange(copies, PLANE)

    blocks, block_cols = lax.optimization_barrier((blocks, block_cols, slices))[:2]
    a00 = build_dense(blocks[:, 0], block_cols[:, 0], block_count[:, 0])
    a01 = swap(a00, "z", LEVELS)
    a10 = swap(a00, "c", CORES)
    a11 = swap(after(a01, whole), "c", CORES)
    panels = (a00, a01, a10, a11)

    hops = []
    for hop in range(HOPS):
        if hop:
            copies = jnp.broadcast_to(sent[None], (plane,) + sent.shape)
            whole = exchange(copies, PLANE)
        stay, go = product(place, whole.reshape(plane, 2, 2 * rows, width), panels)
        come = swap(go, "z", NEIGHBOURS)
        both = (stay.astype(f32) + come.astype(f32)).astype(bf16)
        parts = exchange(both.reshape(STEP, pooled, width), "z", SUM_GROUPS)
        total = jnp.sum(parts.astype(f32), axis=0)
        value = (scale * (total + sent.astype(f32))).astype(bf16)
        sent = (scale * value.astype(f32)).astype(bf16)
        hops.append(value.reshape(4, rows, width))
    back = exchange(jnp.stack(hops, axis=1), ("c", "z"), TILE_GROUPS)
    back = jnp.where(crossed, jnp.roll(back, 2, axis=0), back)
    return tuple(
        back[:, k].transpose(1, 0, 2).reshape(rows, full) for k in range(HOPS)
    )


def solution(mesh):
    axes = tuple(SIZES)
    fine = Mesh(mesh.devices.reshape(tuple(SIZES.values())), axes)
    in_specs = (
        P(axes, None),
        P(axes),
        P(axes[:3], axes[3:], None, None, None),
        P(axes[:3], axes[3:], None),
        P(axes[:3], axes[3:]),
    )
    out_specs = (P(axes, None),) * 3
    return jax.shard_map(
        on_device, mesh=fine, in_specs=in_specs, out_specs=out_specs, check_vma=False
    )
```

```python
import jax
import jax.numpy as jnp
from jax import lax
from jax.experimental import pallas as pl
from jax.experimental.pallas import tpu as pltpu
from jax.sharding import Mesh, PartitionSpec as P

HOPS = 3
SIZES = {"x": 4, "y": 4, "c": 2, "z": 16}
PLANE = ("x", "y")
LENGTH = 16
TILES = LENGTH // 2
STEP = 4
TILE_GROUPS = [
    [core * LENGTH + 2 * k + level for level in range(2) for core in range(2)] for k in range(TILES)
]
NEIGHBOURS = [(z, (z + 1 if z % 2 else z - 1) % LENGTH) for z in range(LENGTH)]
SUM_GROUPS = [
    [(STEP * k + first + (side if k < STEP // 2 else 1 - side)) % LENGTH for k in range(STEP)]
    for first in (1, 3)
    for side in range(2)
]


def tile_order():
    group_of = {z: group for group in SUM_GROUPS for z in group}
    return [[z // 2 for z in group_of[me] + group_of[other]] for me, other in NEIGHBOURS]


LANES = 128
CORES = [(0, 1), (1, 0)]
LEVELS = [(z, z ^ 1) for z in range(LENGTH)]
VMEM = pl.BlockSpec(memory_space=pltpu.VMEM)
SMEM = pl.BlockSpec(memory_space=pltpu.SMEM)


def exchange(x, axes, groups=None):
    return lax.all_to_all(x, axes, 0, 0, tiled=True, axis_index_groups=groups)


def swap(x, axis, pairs):
    return lax.ppermute(x, axis, pairs)


def after(x, *others):
    return lax.optimization_barrier((x,) + others)[0]


def dense_kernel(cols, counts, blocks, out):
    out[...] = jnp.zeros_like(out)
    row_blocks, slots, size, _ = blocks.shape
    for g in range(row_blocks):
        for t in range(slots):

            @pl.when(t < counts[g])
            def _():
                at = pl.multiple_of(cols[g, t] * size, size)
                out[g * size : (g + 1) * size, pl.ds(at, size)] = blocks[g, t]


def build_dense(blocks, cols, counts):
    g, t, size, _ = blocks.shape
    return pl.pallas_call(
        dense_kernel,
        out_shape=jax.ShapeDtypeStruct((g * size, t * size), blocks.dtype),
        in_specs=[SMEM, SMEM, VMEM],
        out_specs=VMEM,
        compiler_params=pltpu.CompilerParams(vmem_limit_bytes=8 << 20),
        name="dense_panel",
    )(cols, counts, blocks)


def product_kernel(begin, place, whole, a00, a01, a10, a11, out, columns):
    core, level = place[0], place[1]
    plane, pair, rows, width = whole.shape
    tile = pair * rows // 2
    for j in range(plane):
        for z in range(pair):
            columns[z, j] = whole[j, z]
    starts = [pl.multiple_of(place[2 + begin + p] * tile, tile) for p in range(STEP)]
    for near, (ours, theirs) in enumerate(((a00, a01), (a10, a11))):
        value = None
        for panel, at in ((ours, level), (theirs, 1 - level)):
            left = jnp.concatenate([panel[pl.ds(start, tile), :] for start in starts])
            right = columns[at].reshape(-1, width)
            part = jnp.dot(left, right, preferred_element_type=jnp.float32)
            value = part if value is None else value + part
        value = value.astype(jnp.bfloat16).reshape(STEP, pair, rows // 2, width)
        target = core if near == 0 else 1 - core
        for z in range(pair):
            out[:, z, target] = value[:, z]


def product(begin, place, whole, panels):
    plane, pair, rows, width = whole.shape

    def body(*refs):
        product_kernel(begin, *refs)

    return pl.pallas_call(
        body,
        out_shape=jax.ShapeDtypeStruct((STEP, pair, 2, rows // 2, width), jnp.bfloat16),
        in_specs=[SMEM] + [VMEM] * 5,
        out_specs=VMEM,
        scratch_shapes=[pltpu.VMEM((pair, plane, rows, width), jnp.bfloat16)],
        compiler_params=pltpu.CompilerParams(vmem_limit_bytes=14 << 20),
        name="go_product" if begin else "stay_product",
    )(place, whole, *panels)


def collect_kernel(crossed, back, *outs):
    _, _, _, width = back.shape
    for q in range(4):
        for k, out in enumerate(outs):
            out[:, q * width : (q + 1) * width] = back[q ^ 2 * crossed[0], k]


def collect(crossed, back):
    _, hops, rows, width = back.shape
    return pl.pallas_call(
        collect_kernel,
        out_shape=(jax.ShapeDtypeStruct((rows, 4 * width), back.dtype),) * hops,
        in_specs=[SMEM, VMEM],
        out_specs=(VMEM,) * hops,
        compiler_params=pltpu.CompilerParams(vmem_limit_bytes=8 << 20),
        name="collect_rows",
    )(crossed, back)


def on_device(features, degree, blocks, block_cols, block_count):
    f32, bf16 = jnp.float32, jnp.bfloat16
    rows, full = features.shape
    width = full // 4
    pooled = 4 * rows
    plane = SIZES["x"] * SIZES["y"]
    z = lax.axis_index("z")
    here = jnp.stack([lax.axis_index("c"), z & 1]).astype(jnp.int32)
    place = jnp.concatenate([here, jnp.asarray(tile_order(), jnp.int32)[z]])
    crossed = (z & 2) != 0

    counts = jnp.broadcast_to(degree.astype(bf16)[:, None], (rows, LANES))
    slices = jnp.stack(
        [
            jnp.concatenate([features[:, q * width : (q + 1) * width], counts], axis=1)
            for q in range(4)
        ]
    )
    slices = jnp.where(crossed, jnp.roll(slices, 2, axis=0), slices)
    got = exchange(slices, ("c", "z"), TILE_GROUPS).reshape(pooled, width + LANES)
    scale = lax.rsqrt(got[:, width : width + 1].astype(f32))
    sent = (scale * got[:, :width].astype(f32)).astype(bf16)
    copies = jnp.broadcast_to(sent[None], (plane,) + sent.shape)
    whole = exchange(copies, PLANE)

    blocks, block_cols = lax.optimization_barrier((blocks, block_cols, slices))[:2]
    a00 = build_dense(blocks[:, 0], block_cols[:, 0], block_count[:, 0])
    a01 = swap(a00, "z", LEVELS)
    a10 = swap(a00, "c", CORES)
    a11 = swap(after(a01, whole), "c", CORES)
    panels = (a00, a01, a10, a11)

    hops = []
    for hop in range(HOPS):
        if hop:
            copies = jnp.broadcast_to(sent[None], (plane,) + sent.shape)
            whole = exchange(copies, PLANE)
        whole = whole.reshape(plane, 2, 2 * rows, width)
        come = swap(product(STEP, place, whole, panels), "z", NEIGHBOURS)
        stay = product(0, place, whole, panels)
        both = (stay.astype(f32) + come.astype(f32)).astype(bf16)
        parts = exchange(both.reshape(STEP, pooled, width), "z", SUM_GROUPS)
        total = jnp.sum(parts.astype(f32), axis=0)
        value = (scale * (total + sent.astype(f32))).astype(bf16)
        sent = (scale * value.astype(f32)).astype(bf16)
        hops.append(value.reshape(4, rows, width))
    back = exchange(jnp.stack(hops, axis=1), ("c", "z"), TILE_GROUPS)
    return collect(((z & 2) >> 1).astype(jnp.int32)[None], back)


def solution(mesh):
    axes = tuple(SIZES)
    fine = Mesh(mesh.devices.reshape(tuple(SIZES.values())), axes)
    in_specs = (
        P(axes, None),
        P(axes),
        P(axes[:3], axes[3:], None, None, None),
        P(axes[:3], axes[3:], None),
        P(axes[:3], axes[3:]),
    )
    out_specs = (P(axes, None),) * 3
    return jax.shard_map(
        on_device, mesh=fine, in_specs=in_specs, out_specs=out_specs, check_vma=False
    )
```

```python
import jax
import jax.numpy as jnp
from jax import lax
from jax.experimental import pallas as pl
from jax.experimental.pallas import tpu as pltpu
from jax.sharding import Mesh, PartitionSpec as P

HOPS = 3
SIZES = {"x": 4, "y": 4, "c": 2, "z": 16}
PLANE = ("x", "y")
LENGTH = 16
TILES = LENGTH // 2
STEP = 4
TILE_GROUPS = [
    [core * LENGTH + 2 * k + level for level in range(2) for core in range(2)] for k in range(TILES)
]
NEIGHBOURS = [(z, (z + 1 if z % 2 else z - 1) % LENGTH) for z in range(LENGTH)]
SUM_GROUPS = [
    [(STEP * k + first + side) % LENGTH for k in range(STEP)]
    for first in (1, 3)
    for side in range(2)
]


def tile_order():
    group_of = {z: group for group in SUM_GROUPS for z in group}
    return [[z // 2 for z in group_of[me] + group_of[other]] for me, other in NEIGHBOURS]


LANES = 128
CORES = [(0, 1), (1, 0)]
LEVELS = [(z, z ^ 1) for z in range(LENGTH)]
VMEM = pl.BlockSpec(memory_space=pltpu.VMEM)
SMEM = pl.BlockSpec(memory_space=pltpu.SMEM)


def exchange(x, axes, groups=None):
    return lax.all_to_all(x, axes, 0, 0, tiled=True, axis_index_groups=groups)


def swap(x, axis, pairs):
    return lax.ppermute(x, axis, pairs)


def after(x, *others):
    return lax.optimization_barrier((x,) + others)[0]


def dense_kernel(cols, counts, blocks, out):
    out[...] = jnp.zeros_like(out)
    row_blocks, slots, size, _ = blocks.shape
    for g in range(row_blocks):
        for t in range(slots):

            @pl.when(t < counts[g])
            def _():
                at = pl.multiple_of(cols[g, t] * size, size)
                out[g * size : (g + 1) * size, pl.ds(at, size)] = blocks[g, t]


def build_dense(blocks, cols, counts):
    g, t, size, _ = blocks.shape
    return pl.pallas_call(
        dense_kernel,
        out_shape=jax.ShapeDtypeStruct((g * size, t * size), blocks.dtype),
        in_specs=[SMEM, SMEM, VMEM],
        out_specs=VMEM,
        compiler_params=pltpu.CompilerParams(vmem_limit_bytes=8 << 20),
        name="dense_panel",
    )(cols, counts, blocks)


def product_kernel(begin, place, whole, a00, a01, a10, a11, out, columns):
    core, level = place[0], place[1]
    plane, pair, rows, width = whole.shape
    tile = pair * rows // 2
    for j in range(plane):
        for z in range(pair):
            columns[z, j] = whole[j, z]
    starts = [pl.multiple_of(place[2 + begin + p] * tile, tile) for p in range(STEP)]
    for near, (ours, theirs) in enumerate(((a00, a01), (a10, a11))):
        value = None
        for panel, at in ((ours, level), (theirs, 1 - level)):
            left = jnp.concatenate([panel[pl.ds(start, tile), :] for start in starts])
            right = columns[at].reshape(-1, width)
            part = jnp.dot(left, right, preferred_element_type=jnp.float32)
            value = part if value is None else value + part
        value = value.astype(jnp.bfloat16).reshape(STEP, pair, rows // 2, width)
        target = core if near == 0 else 1 - core
        for z in range(pair):
            out[:, z, target] = value[:, z]


def product(begin, place, whole, panels):
    plane, pair, rows, width = whole.shape

    def body(*refs):
        product_kernel(begin, *refs)

    return pl.pallas_call(
        body,
        out_shape=jax.ShapeDtypeStruct((STEP, pair, 2, rows // 2, width), jnp.bfloat16),
        in_specs=[SMEM] + [VMEM] * 5,
        out_specs=VMEM,
        scratch_shapes=[pltpu.VMEM((pair, plane, rows, width), jnp.bfloat16)],
        compiler_params=pltpu.CompilerParams(vmem_limit_bytes=14 << 20),
        name="go_product" if begin else "stay_product",
    )(place, whole, *panels)


def collect_kernel(crossed, back, *outs):
    _, _, _, width = back.shape
    for q in range(4):
        for k, out in enumerate(outs):
            out[:, q * width : (q + 1) * width] = back[q ^ 2 * crossed[0], k]


def collect(crossed, back):
    _, hops, rows, width = back.shape
    return pl.pallas_call(
        collect_kernel,
        out_shape=(jax.ShapeDtypeStruct((rows, 4 * width), back.dtype),) * hops,
        in_specs=[SMEM, VMEM],
        out_specs=(VMEM,) * hops,
        compiler_params=pltpu.CompilerParams(vmem_limit_bytes=8 << 20),
        name="collect_rows",
    )(crossed, back)


def on_device(features, degree, blocks, block_cols, block_count):
    f32, bf16 = jnp.float32, jnp.bfloat16
    rows, full = features.shape
    width = full // 4
    pooled = 4 * rows
    plane = SIZES["x"] * SIZES["y"]
    z = lax.axis_index("z")
    here = jnp.stack([lax.axis_index("c"), z & 1]).astype(jnp.int32)
    place = jnp.concatenate([here, jnp.asarray(tile_order(), jnp.int32)[z]])
    crossed = (z & 2) != 0

    counts = jnp.broadcast_to(degree.astype(bf16)[:, None], (rows, LANES))
    slices = jnp.stack(
        [
            jnp.concatenate([features[:, q * width : (q + 1) * width], counts], axis=1)
            for q in range(4)
        ]
    )
    slices = jnp.where(crossed, jnp.roll(slices, 2, axis=0), slices)
    got = exchange(slices, ("c", "z"), TILE_GROUPS).reshape(pooled, width + LANES)
    scale = lax.rsqrt(got[:, width : width + 1].astype(f32))
    sent = (scale * got[:, :width].astype(f32)).astype(bf16)
    copies = jnp.broadcast_to(sent[None], (plane,) + sent.shape)
    whole = exchange(copies, PLANE)

    blocks, block_cols = lax.optimization_barrier((blocks, block_cols, slices))[:2]
    a00 = build_dense(blocks[:, 0], block_cols[:, 0], block_count[:, 0])
    a01 = swap(a00, "z", LEVELS)
    a10 = swap(a00, "c", CORES)
    a11 = swap(after(a01, whole), "c", CORES)
    panels = (a00, a01, a10, a11)

    hops = []
    for hop in range(HOPS):
        if hop:
            copies = jnp.broadcast_to(sent[None], (plane,) + sent.shape)
            whole = exchange(copies, PLANE)
        whole = whole.reshape(plane, 2, 2 * rows, width)
        come = swap(product(STEP, place, whole, panels), "z", NEIGHBOURS)
        stay = product(0, place, whole, panels)
        both = (stay.astype(f32) + come.astype(f32)).astype(bf16)
        parts = exchange(both.reshape(STEP, pooled, width), "z", SUM_GROUPS)
        total = jnp.sum(parts.astype(f32), axis=0)
        value = (scale * (total + sent.astype(f32))).astype(bf16)
        sent = (scale * value.astype(f32)).astype(bf16)
        hops.append(value.reshape(4, rows, width))
    back = exchange(jnp.stack(hops, axis=1), ("c", "z"), TILE_GROUPS)
    return collect(((z & 2) >> 1).astype(jnp.int32)[None], back)


def solution(mesh):
    axes = tuple(SIZES)
    fine = Mesh(mesh.devices.reshape(tuple(SIZES.values())), axes)
    in_specs = (
        P(axes, None),
        P(axes),
        P(axes[:3], axes[3:], None, None, None),
        P(axes[:3], axes[3:], None),
        P(axes[:3], axes[3:]),
    )
    out_specs = (P(axes, None),) * 3
    return jax.shard_map(
        on_device, mesh=fine, in_specs=in_specs, out_specs=out_specs, check_vma=False
    )
```

```python
import jax
import jax.numpy as jnp
from jax import lax
from jax.experimental import pallas as pl
from jax.experimental.pallas import tpu as pltpu
from jax.sharding import Mesh, PartitionSpec as P

HOPS = 3
SIZES = {"x": 4, "y": 4, "c": 2, "z": 16}
PLANE = ("x", "y")
LENGTH = 16
TILES = LENGTH // 2
STEP = 4
TILE_GROUPS = [
    [core * LENGTH + 2 * k + level for level in range(2) for core in range(2)] for k in range(TILES)
]
NEIGHBOURS = [(z, (z + 1 if z % 2 else z - 1) % LENGTH) for z in range(LENGTH)]
SUM_GROUPS = [
    [(STEP * k + first + side) % LENGTH for k in range(STEP)]
    for first in (1, 3)
    for side in range(2)
]


def tile_order():
    group_of = {z: group for group in SUM_GROUPS for z in group}
    return [[z // 2 for z in group_of[me] + group_of[other]] for me, other in NEIGHBOURS]


LANES = 128
CORES = [(0, 1), (1, 0)]
LEVELS = [(z, z ^ 1) for z in range(LENGTH)]
VMEM = pl.BlockSpec(memory_space=pltpu.VMEM)
SMEM = pl.BlockSpec(memory_space=pltpu.SMEM)


def exchange(x, axes, groups=None):
    return lax.all_to_all(x, axes, 0, 0, tiled=True, axis_index_groups=groups)


def swap(x, axis, pairs):
    return lax.ppermute(x, axis, pairs)


def after(x, *others):
    return lax.optimization_barrier((x,) + others)[0]


def dense_kernel(cols, counts, blocks, out):
    out[...] = jnp.zeros_like(out)
    row_blocks, slots, size, _ = blocks.shape
    for g in range(row_blocks):
        for t in range(slots):

            @pl.when(t < counts[g])
            def _():
                at = pl.multiple_of(cols[g, t] * size, size)
                out[g * size : (g + 1) * size, pl.ds(at, size)] = blocks[g, t]


def build_dense(blocks, cols, counts):
    g, t, size, _ = blocks.shape
    return pl.pallas_call(
        dense_kernel,
        out_shape=jax.ShapeDtypeStruct((g * size, t * size), blocks.dtype),
        in_specs=[SMEM, SMEM, VMEM],
        out_specs=VMEM,
        compiler_params=pltpu.CompilerParams(vmem_limit_bytes=8 << 20),
        name="dense_panel",
    )(cols, counts, blocks)


def product_kernel(begin, place, whole, a00, a01, a10, a11, out, columns):
    core, level = place[0], place[1]
    plane, pair, rows, width = whole.shape
    tile = pair * rows // 2
    for j in range(plane):
        for z in range(pair):
            columns[z, j] = whole[j, z]
    starts = [pl.multiple_of(place[2 + begin + p] * tile, tile) for p in range(STEP)]
    for near, (ours, theirs) in enumerate(((a00, a01), (a10, a11))):
        value = None
        for panel, at in ((ours, level), (theirs, 1 - level)):
            left = jnp.concatenate([panel[pl.ds(start, tile), :] for start in starts])
            right = columns[at].reshape(-1, width)
            part = jnp.dot(left, right, preferred_element_type=jnp.float32)
            value = part if value is None else value + part
        value = value.astype(jnp.bfloat16).reshape(STEP, pair, rows // 2, width)
        target = core if near == 0 else 1 - core
        for z in range(pair):
            out[:, z, target] = value[:, z]


def product(begin, place, whole, panels):
    plane, pair, rows, width = whole.shape

    def body(*refs):
        product_kernel(begin, *refs)

    return pl.pallas_call(
        body,
        out_shape=jax.ShapeDtypeStruct((STEP, pair, 2, rows // 2, width), jnp.bfloat16),
        in_specs=[SMEM] + [VMEM] * 5,
        out_specs=VMEM,
        scratch_shapes=[pltpu.VMEM((pair, plane, rows, width), jnp.bfloat16)],
        compiler_params=pltpu.CompilerParams(vmem_limit_bytes=14 << 20),
        name="go_product" if begin else "stay_product",
    )(place, whole, *panels)


def collect_kernel(crossed, early, late, *outs):
    _, n_early, _, width = early.shape
    for q in range(4):
        at = q ^ 2 * crossed[0]
        for k, out in enumerate(outs):
            part = early[at, k] if k < n_early else late[at, k - n_early]
            out[:, q * width : (q + 1) * width] = part


def collect(crossed, early, late):
    _, n_early, rows, width = early.shape
    hops = n_early + late.shape[1]
    return pl.pallas_call(
        collect_kernel,
        out_shape=(jax.ShapeDtypeStruct((rows, 4 * width), early.dtype),) * hops,
        in_specs=[SMEM, VMEM, VMEM],
        out_specs=(VMEM,) * hops,
        compiler_params=pltpu.CompilerParams(vmem_limit_bytes=8 << 20),
        name="collect_rows",
    )(crossed, early, late)


def on_device(features, degree, blocks, block_cols, block_count):
    f32, bf16 = jnp.float32, jnp.bfloat16
    rows, full = features.shape
    width = full // 4
    pooled = 4 * rows
    plane = SIZES["x"] * SIZES["y"]
    z = lax.axis_index("z")
    here = jnp.stack([lax.axis_index("c"), z & 1]).astype(jnp.int32)
    place = jnp.concatenate([here, jnp.asarray(tile_order(), jnp.int32)[z]])
    crossed = (z & 2) != 0

    counts = jnp.broadcast_to(degree.astype(bf16)[:, None], (rows, LANES))
    slices = jnp.stack(
        [
            jnp.concatenate([features[:, q * width : (q + 1) * width], counts], axis=1)
            for q in range(4)
        ]
    )
    slices = jnp.where(crossed, jnp.roll(slices, 2, axis=0), slices)
    got = exchange(slices, ("c", "z"), TILE_GROUPS).reshape(pooled, width + LANES)
    scale = lax.rsqrt(got[:, width : width + 1].astype(f32))
    sent = (scale * got[:, :width].astype(f32)).astype(bf16)
    copies = jnp.broadcast_to(sent[None], (plane,) + sent.shape)
    whole = exchange(copies, PLANE)

    blocks, block_cols = lax.optimization_barrier((blocks, block_cols, slices))[:2]
    a00 = build_dense(blocks[:, 0], block_cols[:, 0], block_count[:, 0])
    a01 = swap(a00, "z", LEVELS)
    a10 = swap(a00, "c", CORES)
    a11 = swap(after(a01, whole), "c", CORES)
    panels = (a00, a01, a10, a11)

    hops = []
    for hop in range(HOPS):
        if hop:
            copies = jnp.broadcast_to(sent[None], (plane,) + sent.shape)
            whole = exchange(copies, PLANE)
        whole = whole.reshape(plane, 2, 2 * rows, width)
        go = product(STEP, place, whole, panels)
        come = swap(go, "z", NEIGHBOURS)
        if hop == HOPS - 1:
            early = exchange(after(jnp.stack(hops, axis=1), go), ("c", "z"), TILE_GROUPS)
        stay = product(0, place, whole, panels)
        if hop == HOPS - 1:
            stay = after(stay, early)
        both = (stay.astype(f32) + come.astype(f32)).astype(bf16)
        parts = exchange(both.reshape(STEP, pooled, width), "z", SUM_GROUPS)
        total = jnp.sum(parts.astype(f32), axis=0)
        value = (scale * (total + sent.astype(f32))).astype(bf16)
        sent = (scale * value.astype(f32)).astype(bf16)
        hops.append(value.reshape(4, rows, width))
    late = exchange(hops[-1], ("c", "z"), TILE_GROUPS)[:, None]
    return collect(((z & 2) >> 1).astype(jnp.int32)[None], early, late)


def solution(mesh):
    axes = tuple(SIZES)
    fine = Mesh(mesh.devices.reshape(tuple(SIZES.values())), axes)
    in_specs = (
        P(axes, None),
        P(axes),
        P(axes[:3], axes[3:], None, None, None),
        P(axes[:3], axes[3:], None),
        P(axes[:3], axes[3:]),
    )
    out_specs = (P(axes, None),) * 3
    return jax.shard_map(
        on_device, mesh=fine, in_specs=in_specs, out_specs=out_specs, check_vma=False
    )
```

```python
import jax
import jax.numpy as jnp
from jax import lax
from jax.experimental import pallas as pl
from jax.experimental.pallas import tpu as pltpu
from jax.sharding import Mesh, PartitionSpec as P

HOPS = 3
SIZES = {"x": 4, "y": 4, "c": 2, "z": 16}
PLANE = ("x", "y")
LENGTH = 16
TILES = LENGTH // 2
STEP = 4
TILE_GROUPS = [
    [core * LENGTH + 2 * k + level for level in range(2) for core in range(2)] for k in range(TILES)
]
NEIGHBOURS = [(z, (z + 1 if z % 2 else z - 1) % LENGTH) for z in range(LENGTH)]
SIDES = ((0, 0, 1, 1), (0, 1, 1, 0))
SUM_GROUPS = [
    [core * LENGTH + (STEP * k + first + (side ^ SIDES[core][k])) % LENGTH for k in range(STEP)]
    for core in range(2)
    for first in (1, 3)
    for side in range(2)
]


def tile_order():
    group_of = {device: group for group in SUM_GROUPS for device in group}
    return [
        [
            device % LENGTH // 2
            for z in (me, other)
            for device in group_of[core * LENGTH + z]
        ]
        for core in range(2)
        for me, other in NEIGHBOURS
    ]


LANES = 128
CORES = [(0, 1), (1, 0)]
LEVELS = [(z, z ^ 1) for z in range(LENGTH)]
VMEM = pl.BlockSpec(memory_space=pltpu.VMEM)
SMEM = pl.BlockSpec(memory_space=pltpu.SMEM)


def exchange(x, axes, groups=None):
    return lax.all_to_all(x, axes, 0, 0, tiled=True, axis_index_groups=groups)


def swap(x, axis, pairs):
    return lax.ppermute(x, axis, pairs)


def after(x, *others):
    return lax.optimization_barrier((x,) + others)[0]


def dense_kernel(cols, counts, blocks, out):
    out[...] = jnp.zeros_like(out)
    row_blocks, slots, size, _ = blocks.shape
    for g in range(row_blocks):
        for t in range(slots):

            @pl.when(t < counts[g])
            def _():
                at = pl.multiple_of(cols[g, t] * size, size)
                out[g * size : (g + 1) * size, pl.ds(at, size)] = blocks[g, t]


def build_dense(blocks, cols, counts):
    g, t, size, _ = blocks.shape
    return pl.pallas_call(
        dense_kernel,
        out_shape=jax.ShapeDtypeStruct((g * size, t * size), blocks.dtype),
        in_specs=[SMEM, SMEM, VMEM],
        out_specs=VMEM,
        compiler_params=pltpu.CompilerParams(vmem_limit_bytes=8 << 20),
        name="dense_panel",
    )(cols, counts, blocks)


def product_kernel(begin, place, whole, a00, a01, a10, a11, out, columns):
    core, level = place[0], place[1]
    plane, pair, rows, width = whole.shape
    tile = pair * rows // 2
    for j in range(plane):
        for z in range(pair):
            columns[z, j] = whole[j, z]
    starts = [pl.multiple_of(place[2 + begin + p] * tile, tile) for p in range(STEP)]
    for near, (ours, theirs) in enumerate(((a00, a01), (a10, a11))):
        value = None
        for panel, at in ((ours, level), (theirs, 1 - level)):
            left = jnp.concatenate([panel[pl.ds(start, tile), :] for start in starts])
            right = columns[at].reshape(-1, width)
            part = jnp.dot(left, right, preferred_element_type=jnp.float32)
            value = part if value is None else value + part
        value = value.astype(jnp.bfloat16).reshape(STEP, pair, rows // 2, width)
        target = core if near == 0 else 1 - core
        for z in range(pair):
            out[:, z, target] = value[:, z]


def product(begin, place, whole, panels):
    plane, pair, rows, width = whole.shape

    def body(*refs):
        product_kernel(begin, *refs)

    return pl.pallas_call(
        body,
        out_shape=jax.ShapeDtypeStruct((STEP, pair, 2, rows // 2, width), jnp.bfloat16),
        in_specs=[SMEM] + [VMEM] * 5,
        out_specs=VMEM,
        scratch_shapes=[pltpu.VMEM((pair, plane, rows, width), jnp.bfloat16)],
        compiler_params=pltpu.CompilerParams(vmem_limit_bytes=14 << 20),
        name="go_product" if begin else "stay_product",
    )(place, whole, *panels)


def collect_kernel(crossed, back, *outs):
    _, _, _, width = back.shape
    for q in range(4):
        for k, out in enumerate(outs):
            out[:, q * width : (q + 1) * width] = back[q ^ 2 * crossed[0], k]


def collect(crossed, back):
    _, hops, rows, width = back.shape
    return pl.pallas_call(
        collect_kernel,
        out_shape=(jax.ShapeDtypeStruct((rows, 4 * width), back.dtype),) * hops,
        in_specs=[SMEM, VMEM],
        out_specs=(VMEM,) * hops,
        compiler_params=pltpu.CompilerParams(vmem_limit_bytes=8 << 20),
        name="collect_rows",
    )(crossed, back)


def on_device(features, degree, blocks, block_cols, block_count):
    f32, bf16 = jnp.float32, jnp.bfloat16
    rows, full = features.shape
    width = full // 4
    pooled = 4 * rows
    plane = SIZES["x"] * SIZES["y"]
    z = lax.axis_index("z")
    here = jnp.stack([lax.axis_index("c"), z & 1]).astype(jnp.int32)
    place = jnp.concatenate([here, jnp.asarray(tile_order(), jnp.int32)[lax.axis_index("c") * LENGTH + z]])
    crossed = (z & 2) != 0

    counts = jnp.broadcast_to(degree.astype(bf16)[:, None], (rows, LANES))
    slices = jnp.stack(
        [
            jnp.concatenate([features[:, q * width : (q + 1) * width], counts], axis=1)
            for q in range(4)
        ]
    )
    slices = jnp.where(crossed, jnp.roll(slices, 2, axis=0), slices)
    got = exchange(slices, ("c", "z"), TILE_GROUPS).reshape(pooled, width + LANES)
    scale = lax.rsqrt(got[:, width : width + 1].astype(f32))
    sent = (scale * got[:, :width].astype(f32)).astype(bf16)
    copies = jnp.broadcast_to(sent[None], (plane,) + sent.shape)
    whole = exchange(copies, PLANE)

    blocks, block_cols = lax.optimization_barrier((blocks, block_cols, slices))[:2]
    a00 = build_dense(blocks[:, 0], block_cols[:, 0], block_count[:, 0])
    a01 = swap(a00, "z", LEVELS)
    a10 = swap(a00, "c", CORES)
    a11 = swap(after(a01, whole), "c", CORES)
    panels = (a00, a01, a10, a11)

    hops = []
    for hop in range(HOPS):
        if hop:
            copies = jnp.broadcast_to(sent[None], (plane,) + sent.shape)
            whole = exchange(copies, PLANE)
        whole = whole.reshape(plane, 2, 2 * rows, width)
        come = swap(product(STEP, place, whole, panels), "z", NEIGHBOURS)
        stay = product(0, place, whole, panels)
        both = (stay.astype(f32) + come.astype(f32)).astype(bf16)
        parts = exchange(both.reshape(STEP, pooled, width), ("c", "z"), SUM_GROUPS)
        total = jnp.sum(parts.astype(f32), axis=0)
        value = (scale * (total + sent.astype(f32))).astype(bf16)
        sent = (scale * value.astype(f32)).astype(bf16)
        hops.append(value.reshape(4, rows, width))
    back = exchange(jnp.stack(hops, axis=1), ("c", "z"), TILE_GROUPS)
    return collect(((z & 2) >> 1).astype(jnp.int32)[None], back)


def solution(mesh):
    axes = tuple(SIZES)
    fine = Mesh(mesh.devices.reshape(tuple(SIZES.values())), axes)
    in_specs = (
        P(axes, None),
        P(axes),
        P(axes[:3], axes[3:], None, None, None),
        P(axes[:3], axes[3:], None),
        P(axes[:3], axes[3:]),
    )
    out_specs = (P(axes, None),) * 3
    return jax.shard_map(
        on_device, mesh=fine, in_specs=in_specs, out_specs=out_specs, check_vma=False
    )
```
